32 devices in a mesh: space: 8 (over y, x, core), sample: 4 (over z).
Axes of the slice: x: 2, y: 2, z: 4, core: 2. Of those that a mesh axis runs over, the one named last changes fastest.
Arguments:
- fields: bfloat16 [4, 64, 20, 8192], P('sample', 'space'), may hold values from -6 to 6
- cotangent: bfloat16 [4, 64, 20, 8192], P('sample', 'space'), may hold values from -6 to 6
- spectral_weight: bfloat16 [2, 20, 20, 4608], P(None, None, None, 'space'), may hold values from -6 to 6
- point_weight: bfloat16 [20, 20], replicated, may hold values from -1.25 to 1.25
- point_bias: float32 [20], replicated, may hold values from -1 to 1
Outputs:
- activated: bfloat16 [4, 64, 20, 8192], P('sample', 'space')
- grad_input: bfloat16 [4, 64, 20, 8192], P('sample', 'space')
- grad_spectral: float32 [2, 20, 20, 4608], P(None, None, None, ('space', 'sample'))
The draws below stay inside these ranges and needn't reach their ends.
All inputs are finite; a program needn't handle non-finite values.
Results may differ from the reference program's by a relative error of at most 0.001.
Values sent between devices are 32-bit elements; how exact they have to be, the bound alone decides.
A program may use at most 128 MiB of HBM per device.

```python
import math
import jax
import jax.numpy as jnp
from jax import lax

NX = 64
NY = 64
NZ = 32
NT = 4
C = 20
MX = 12
MY = 12
MZ = 8
MT = 4
SAMPLES = 4
CELLS = 8192
MODES = 4608


def level_of(stream_key, extent, cuts, smallest, top_value):
    gain, own = 1.0, jax.random.fold_in(stream_key, 6)
    for axis_at, blocks in cuts:
        steps = jnp.exp(jax.random.uniform(jax.random.fold_in(own, axis_at), (blocks,), jnp.float32, smallest / len(cuts), top_value / len(cuts)))
        gain = gain * jnp.repeat(steps, extent[axis_at] // blocks).reshape([-1 if axis == axis_at else 1 for axis in range(len(extent))])
    return gain


def scatter_about(own_key, extent, width, limit, pieces=(), kind=jnp.bfloat16):
    factor_of = level_of(own_key, extent, pieces, -0.22, 0.18) if pieces else 1.0
    result = jax.random.normal(own_key, extent, jnp.float32) * width * factor_of
    return jnp.minimum(jnp.maximum(result, -limit), limit).astype(kind)


def setup_inputs(seed: int = 0) -> dict:
    arg_keys = jax.random.split(jax.random.key(seed), 6)
    return {
        "fields": scatter_about(arg_keys[0], (SAMPLES, NX, C, CELLS), 1.0, 6.0, ((0, 4), (1, 8))),
        "cotangent": scatter_about(arg_keys[1], (SAMPLES, NX, C, CELLS), 1.0, 6.0, ((0, 4), (1, 8))),
        "spectral_weight": scatter_about(arg_keys[2], (2, C, C, MODES), 1.0, 6.0, ((3, 8),)),
        "point_weight": scatter_about(arg_keys[3], (C, C), C ** -0.5, 1.25),
        "point_bias": jnp.clip(jax.random.uniform(arg_keys[4], (C,), jnp.float32, -1.0, 1.0), -1.0, 1.0),
    }


def kept_index(length, modes):
    index = jnp.arange(modes, dtype=jnp.int32)
    return jnp.where(index < modes // 2, index, length - modes + index)

def mode_indices():
    index_x = kept_index(NX, MX)[:, None, None, None]
    index_y = kept_index(NY, MY)[None, :, None, None]
    index_z = kept_index(NZ, MZ)[None, None, :, None]
    index_t = kept_index(NT, MT)[None, None, None, :]
    return (index_x, index_y, index_z, index_t)

def to_grid(planes):
    return jnp.transpose(planes, (1, 0, 2)).reshape(planes.shape[1], NX, NY, NZ, NT)

def from_grid(lattice):
    return jnp.transpose(lattice.reshape(lattice.shape[0], NX, NY * NZ * NT), (1, 0, 2))

def select_modes(spectrum):
    index_x, index_y, index_z, index_t = mode_indices()
    picked = spectrum[:, index_x, index_y, index_z, index_t]
    return jnp.transpose(picked, (0, 3, 4, 2, 1)).reshape(spectrum.shape[0], MZ * MT * MY * MX)

def place_modes(coeffs):
    index_x, index_y, index_z, index_t = mode_indices()
    arranged = jnp.transpose(coeffs.reshape(coeffs.shape[0], MZ, MT, MY, MX), (0, 4, 3, 1, 2))
    empty = jnp.zeros((coeffs.shape[0], NX, NY, NZ, NT), dtype=coeffs.dtype)
    return empty.at[:, index_x, index_y, index_z, index_t].set(arranged)

def gelu_slope(values):
    return 0.5 * (1.0 + lax.erf(values * (1.0 / math.sqrt(2.0)))) + values * jnp.exp(-0.5 * values * values) * (1.0 / math.sqrt(2.0 * math.pi))

def reference(fields, cotangent, spectral_weight, point_weight, point_bias):
    volume = NX * NY * NZ * NT
    weights = spectral_weight.astype(jnp.float32)
    mixer_full = weights[0] + 1j * weights[1]
    mixer_conj = weights[0] - 1j * weights[1]
    point_mat = point_weight.astype(jnp.float32)
    bias_vec = point_bias.astype(jnp.float32)
    highest = lax.Precision.HIGHEST

    def per_sample(running, inputs_pair):
        sample_field, sample_cot = inputs_pair
        values = sample_field.astype(jnp.float32)
        spec_in = select_modes(jnp.fft.fftn(to_grid(values), axes=(1, 2, 3, 4)))
        mixed = jnp.einsum('com,cm->om', mixer_full, spec_in, precision=highest)
        spectral = from_grid(jnp.real(jnp.fft.ifftn(place_modes(mixed), axes=(1, 2, 3, 4))))
        local = jnp.einsum('xcn,co->xon', values, point_mat, precision=highest)
        pre = spectral + local + bias_vec[None, :, None]
        activated = jax.nn.gelu(pre, approximate=False).astype(jnp.bfloat16)
        upstream = sample_cot.astype(jnp.float32) * gelu_slope(pre)
        spec_up = select_modes(jnp.fft.fftn(to_grid(upstream), axes=(1, 2, 3, 4))) / volume
        back = jnp.einsum('com,om->cm', mixer_conj, spec_up, precision=highest)
        spectral_back = from_grid(jnp.real(jnp.fft.ifftn(place_modes(back), axes=(1, 2, 3, 4)))) * volume
        grad_in = (spectral_back + jnp.einsum('xon,co->xcn', upstream, point_mat, precision=highest)).astype(jnp.bfloat16)
        grad_term = jnp.conj(spec_in)[:, None, :] * spec_up[None, :, :]
        running = running + jnp.stack([jnp.real(grad_term), jnp.imag(grad_term)]).astype(jnp.float32)
        return (running, (activated, grad_in))
    initial = jnp.zeros((2, C, C, MZ * MT * MY * MX), jnp.float32)
    running, outputs = lax.scan(per_sample, initial, (fields, cotangent))
    return (outputs[0], outputs[1], running)
```

```python
import math

import jax
import jax.numpy as jnp
import numpy as np
from jax import lax
from jax.experimental import pallas as pl
from jax.experimental.pallas import tpu as pltpu
from jax.sharding import PartitionSpec as P

NX, NY, NZ, NT = 64, 64, 32, 4
MX, MY, MZ, MT = 12, 12, 8, 4
VOLUME = NX * NY * NZ * NT
PLANE = NZ * NT
XY = MX * MY
BF16, F32 = jnp.bfloat16, jnp.float32
VMEM_LIMIT = 60 * 1024 * 1024


def signed(modes):
    index = np.arange(modes)
    return np.where(index < modes // 2, index, index - modes)


def split_np(table):
    high = table.astype(np.float32).astype(BF16)
    low = (table - high.astype(np.float64)).astype(np.float32).astype(BF16)
    return high, low


def tables(rows, space):
    y, x = np.arange(NY)[:, None], np.arange(rows)[None, :]
    fy, fx = signed(MY)[:, None], signed(MX)[None, :]
    phi = 2 * np.pi * (
        fy.reshape(MY, 1, 1, 1) * y.reshape(1, 1, NY, 1) / NY
        + fx.reshape(1, MX, 1, 1) * x.reshape(1, 1, 1, rows) / NX
    ).reshape(XY, NY * rows)
    plane = np.concatenate([np.cos(phi), np.sin(phi)], 0)
    hi, lo = split_np(plane)
    forward = np.concatenate([hi, lo], 0)
    inverse = np.concatenate([hi.T, lo.T], 0)
    fz, ft = signed(MZ), signed(MT)
    z, t = np.arange(NZ), np.arange(NT)
    psi = 2 * np.pi * (
        fz.reshape(MZ, 1, 1, 1) * z.reshape(1, 1, NZ, 1) / NZ
        + ft.reshape(1, MT, 1, 1) * t.reshape(1, 1, 1, NT) / NT
    ).reshape(space, MZ * MT // space, PLANE)
    cos, sin = np.cos(psi), np.sin(psi)
    depth = np.stack(
        [np.concatenate([cos, -sin], -1), np.concatenate([-sin, -cos], -1)], 1
    ).reshape(MZ * 2 * MT, 2 * PLANE)
    dhi, dlo = split_np(depth)
    depth_forward = np.concatenate([dhi, dlo], 0)
    depth_inverse = np.concatenate([dhi, dhi, dlo], 0)
    return forward, inverse, depth_forward, depth_inverse


def split(value):
    high = value.astype(BF16)
    return high, (value - high.astype(F32)).astype(BF16)


def dot(a, b):
    return lax.dot_general(a, b, (((1,), (0,)), ((), ())), preferred_element_type=F32)


def forward_transform(src, fwd, depth, zhi, zlo, out, exact):
    channels = src.shape[0]
    half = fwd.shape[0] // 2

    def pair(g, carry):
        block = jnp.concatenate([src[2 * g], src[2 * g + 1]], -1)
        if exact:
            res = dot(fwd[...], block.astype(BF16))
            res = res[:half] + res[half:]
        else:
            high, low = split(block)
            res = dot(fwd[...], high)
            res = res[:half] + res[half:] + dot(fwd[:half], low)
        for k in range(2):
            part = res[:, k * PLANE : (k + 1) * PLANE]
            high, low = split(jnp.concatenate([part[:XY], part[XY:]], -1))
            zhi[2 * g + k] = high
            zlo[2 * g + k] = low
        return carry

    lax.fori_loop(0, channels // 2, pair, 0)
    rows = out.shape[0]
    contract = (((1,), (1,)), ((), ()))
    high = zhi[...].reshape(channels * XY, 2 * PLANE)
    low = zlo[...].reshape(channels * XY, 2 * PLANE)
    first = lax.dot_general(depth[...], high, contract, preferred_element_type=F32)
    second = lax.dot_general(depth[:rows], low, contract, preferred_element_type=F32)
    out[...] = first[:rows] + first[rows:] + second


def inverse_transform(modes, depth, inv, ghi, glo, dst):
    outputs = dst.shape[0]
    cells = inv.shape[0] // 2
    high, low = split(modes[...])
    stacked = jnp.concatenate([high, low, high], 0)
    lines = lax.dot_general(
        stacked, depth[...], (((0,), (0,)), ((), ())), preferred_element_type=F32
    )
    high, low = split(lines.reshape(outputs, XY, 2 * PLANE))
    ghi[:, :XY] = high[:, :, :PLANE]
    ghi[:, XY:] = high[:, :, PLANE:]
    glo[:, :XY] = low[:, :, :PLANE]
    glo[:, XY:] = low[:, :, PLANE:]

    def pair(g, carry):
        high = jnp.concatenate([ghi[2 * g], ghi[2 * g + 1]], -1)
        low = jnp.concatenate([glo[2 * g], glo[2 * g + 1]], -1)
        res = dot(inv[...], high)
        res = res[:cells] + res[cells:] + dot(inv[:cells], low)
        dst[2 * g] = res[:, :PLANE]
        dst[2 * g + 1] = res[:, PLANE:]
        return carry

    lax.fori_loop(0, outputs // 2, pair, 0)


def first_kernel(fields, fwd, depth, out, src, zhi, zlo):
    rows = fields.shape[1]

    def line(i, carry):
        at = pl.multiple_of(i * PLANE, PLANE)
        to = pl.multiple_of(i * rows, rows)
        src[:, pl.ds(to, rows), :] = fields[:, :, pl.ds(at, PLANE)].astype(F32)
        return carry

    lax.fori_loop(0, NY, line, 0)
    forward_transform(src, fwd, depth, zhi, zlo, out, True)


def middle_kernel(
    modes, fields, cot, mix, mix_back, bias, fwd, inv, depth, depth_inv,
    activated, local, out, work, ghi, glo, zhi, zlo,
):
    channels, rows, _ = fields.shape
    inverse_transform(modes, depth_inv, inv, ghi, glo, work)
    flat = channels * rows

    def line(i, carry):
        at = pl.multiple_of(i * 2 * PLANE, 2 * PLANE)
        block = fields[:, :, pl.ds(at, 2 * PLANE)].astype(F32)
        near = dot(mix[...], block.reshape(flat, 2 * PLANE).astype(BF16))
        ups = []
        for k in range(2):
            here = pl.multiple_of(at + k * PLANE, PLANE)
            to = pl.multiple_of((2 * i + k) * rows, rows)
            far = work[:, pl.ds(to, rows), :].reshape(flat, PLANE)
            pre = far + near[:, k * PLANE : (k + 1) * PLANE] + bias[...]
            phi = 0.5 * (1.0 + lax.erf(pre * (1.0 / math.sqrt(2.0))))
            slope = phi + pre * jnp.exp(-0.5 * pre * pre) * (1.0 / math.sqrt(2.0 * math.pi))
            act = (pre * phi).reshape(channels, rows, PLANE)
            activated[:, :, pl.ds(here, PLANE)] = act.astype(BF16)
            c = cot[:, :, pl.ds(here, PLANE)].astype(F32).reshape(flat, PLANE)
            up = c * slope
            work[:, pl.ds(to, rows), :] = up.reshape(channels, rows, PLANE)
            ups.append(up)
        high, low = split(jnp.concatenate(ups, -1))
        back = dot(mix_back[...], high) + dot(mix_back[...], low)
        local[:, :, pl.ds(at, 2 * PLANE)] = back.reshape(channels, rows, 2 * PLANE)
        return carry

    lax.fori_loop(0, NY // 2, line, 0)
    forward_transform(work, fwd, depth, zhi, zlo, out, False)


def last_kernel(modes, local, inv, depth_inv, out, work, ghi, glo):
    rows = local.shape[1]
    inverse_transform(modes, depth_inv, inv, ghi, glo, work)

    def line(i, carry):
        at = pl.multiple_of(i * PLANE, PLANE)
        to = pl.multiple_of(i * rows, rows)
        value = work[:, pl.ds(to, rows), :] + local[:, :, pl.ds(at, PLANE)]
        out[:, :, pl.ds(at, PLANE)] = value.astype(BF16)
        return carry

    lax.fori_loop(0, NY, line, 0)


def call(body, outs, scratch):
    return pl.pallas_call(
        body,
        out_shape=outs,
        scratch_shapes=scratch,
        compiler_params=pltpu.CompilerParams(vmem_limit_bytes=VMEM_LIMIT),
    )


def shards(fields, cotangent, spectral_weight, point_weight, point_bias):
    _, rows, channels, columns = fields.shape
    space = lax.axis_size("space")
    samples = lax.axis_size("sample")
    fwd, inv, depth, depth_inv = [jnp.asarray(t) for t in tables(rows, space)]
    owned = MT * MZ // space
    own_rows = 2 * owned
    all_rows = 2 * MT * MZ
    lanes = channels * XY
    cells = NY * rows
    field = jnp.transpose(fields[0], (1, 0, 2))
    cot = jnp.transpose(cotangent[0], (1, 0, 2))
    eye = jnp.eye(rows, dtype=BF16)
    flat = channels * rows
    mix_back = (point_weight[:, None, :, None] * eye[None, :, None, :]).reshape(flat, flat)
    mix = (point_weight.T[:, None, :, None] * eye[None, :, None, :]).reshape(flat, flat)
    bias = jnp.broadcast_to(point_bias[:, None, None], (channels, rows, PLANE)).reshape(flat, PLANE)

    freq = np.tile(signed(MX), MY * channels)
    angle = 2 * np.pi * (freq[None, :] * np.arange(space)[:, None] * rows % NX) / NX
    turn_cos = np.cos(angle).astype(np.float32)
    turn_sin = np.sin(angle).astype(np.float32)

    z_buf = pltpu.VMEM((channels, XY, 2 * PLANE), BF16)
    g_buf = pltpu.VMEM((channels, 2 * XY, PLANE), BF16)
    w_buf = pltpu.VMEM((channels, cells, PLANE), F32)
    part = jax.ShapeDtypeStruct((all_rows, lanes), F32)
    grid_bf = jax.ShapeDtypeStruct((channels, rows, columns), BF16)
    grid_f = jax.ShapeDtypeStruct((channels, rows, columns), F32)

    def to_owner(partial):
        got = lax.all_to_all(
            partial.reshape(space, own_rows, lanes), "space", 0, 0, tiled=True
        ).reshape(space, 2, owned, lanes)
        cos, sin = turn_cos[:, None, :], turn_sin[:, None, :]
        real, imag = got[:, 0], got[:, 1]
        out_r = jnp.sum(real * cos + imag * sin, 0)
        out_i = jnp.sum(imag * cos - real * sin, 0)
        both = jnp.stack([out_r, out_i]).reshape(2, owned, channels, XY)
        return jnp.transpose(both, (0, 2, 1, 3)).reshape(2, channels, -1)

    me = lax.axis_index("space")
    my_cos = lax.dynamic_slice_in_dim(jnp.asarray(turn_cos), me, 1, 0)
    my_sin = lax.dynamic_slice_in_dim(jnp.asarray(turn_sin), me, 1, 0)

    def to_slab(real, imag, scale):
        both = jnp.stack([real, imag]).reshape(2, channels, owned, XY)
        send = jnp.transpose(both, (0, 2, 1, 3)).reshape(own_rows, lanes)
        got = lax.all_to_all(
            jnp.broadcast_to(send[None], (space, own_rows, lanes)), "space", 0, 0, tiled=True
        ).reshape(space, 2, owned, lanes)
        cos, sin = my_cos * scale, my_sin * scale
        out_r = got[:, 0] * cos - got[:, 1] * sin
        out_i = got[:, 0] * sin + got[:, 1] * cos
        return jnp.stack([out_r, out_i], 1).reshape(all_rows, lanes)

    weights = spectral_weight.astype(F32)
    w_r, w_i = weights[0], weights[1]

    partial = call(first_kernel, part, [w_buf, z_buf, z_buf])(field, fwd, depth)
    s_r, s_i = to_owner(partial)
    mixed_r = jnp.sum(w_r * s_r[:, None] - w_i * s_i[:, None], 0)
    mixed_i = jnp.sum(w_r * s_i[:, None] + w_i * s_r[:, None], 0)
    modes = to_slab(mixed_r, mixed_i, 1.0 / VOLUME)
    activated, local, partial_up = call(
        middle_kernel, (grid_bf, grid_f, part), [w_buf, g_buf, g_buf, z_buf, z_buf]
    )(modes, field, cot, mix, mix_back, bias, fwd, inv, depth, depth_inv)
    u_r, u_i = to_owner(partial_up)
    u_r, u_i = u_r * (1.0 / VOLUME), u_i * (1.0 / VOLUME)
    back_r = jnp.sum(w_r * u_r[None] + w_i * u_i[None], 1)
    back_i = jnp.sum(w_r * u_i[None] - w_i * u_r[None], 1)
    modes_back = to_slab(back_r, back_i, 1.0)
    grad_input = call(last_kernel, grid_bf, [w_buf, g_buf, g_buf])(
        modes_back, local, inv, depth_inv
    )

    factors = jnp.stack([s_r, s_i, u_r, u_i]).reshape(4 * channels, samples, -1)
    factors = jnp.transpose(factors, (1, 0, 2))
    factors = lax.all_to_all(factors, "sample", 0, 0, tiled=True)
    factors = factors.reshape(samples, 4, channels, -1)
    a_r, a_i = factors[:, 0, :, None], factors[:, 1, :, None]
    b_r, b_i = factors[:, 2, None], factors[:, 3, None]
    grad_r = sum(a_r[s] * b_r[s] + a_i[s] * b_i[s] for s in range(samples))
    grad_i = sum(a_r[s] * b_i[s] - a_i[s] * b_r[s] for s in range(samples))
    grad_spectral = jnp.stack([grad_r, grad_i])
    back_to = lambda value: jnp.transpose(value, (1, 0, 2))[None]
    return back_to(activated), back_to(grad_input), grad_spectral


def solution(mesh):
    return jax.shard_map(
        shards,
        mesh=mesh,
        in_specs=(
            P("sample", "space", None, None),
            P("sample", "space", None, None),
            P(None, None, None, "space"),
            P(),
            P(),
        ),
        out_specs=(
            P("sample", "space", None, None),
            P("sample", "space", None, None),
            P(None, None, None, ("space", "sample")),
        ),
        check_vma=False,
    )
```

```python
import functools
import math

import jax
import jax.numpy as jnp
import numpy as np
from jax import lax
from jax.experimental import pallas as pl
from jax.experimental.pallas import tpu as pltpu
from jax.sharding import PartitionSpec as P

NX, NY, NZ, NT = 64, 64, 32, 4
MX, MY, MZ, MT = 12, 12, 8, 4
VOLUME = NX * NY * NZ * NT
PLANE = NZ * NT
XY = MX * MY
BF16, F32 = jnp.bfloat16, jnp.float32
VMEM_LIMIT = 60 * 1024 * 1024


def signed(modes):
    index = np.arange(modes)
    return np.where(index < modes // 2, index, index - modes)


def split_np(table):
    high = table.astype(np.float32).astype(BF16)
    low = (table - high.astype(np.float64)).astype(np.float32).astype(BF16)
    return high, low


def tables(rows, space):
    y, x = np.arange(NY)[:, None], np.arange(rows)[None, :]
    fy, fx = signed(MY)[:, None], signed(MX)[None, :]
    phi = 2 * np.pi * (
        fy.reshape(MY, 1, 1, 1) * y.reshape(1, 1, NY, 1) / NY
        + fx.reshape(1, MX, 1, 1) * x.reshape(1, 1, 1, rows) / NX
    ).reshape(XY, NY * rows)
    plane = np.concatenate([np.cos(phi), np.sin(phi)], 0)
    hi, lo = split_np(plane)
    forward = np.concatenate([hi, lo], 0)
    inverse = np.concatenate([hi.T, lo.T], 0)
    fz, ft = signed(MZ), signed(MT)
    z, t = np.arange(NZ), np.arange(NT)
    psi = 2 * np.pi * (
        fz.reshape(MZ, 1, 1, 1) * z.reshape(1, 1, NZ, 1) / NZ
        + ft.reshape(1, MT, 1, 1) * t.reshape(1, 1, 1, NT) / NT
    ).reshape(space, MZ * MT // space, PLANE)
    cos, sin = np.cos(psi), np.sin(psi)
    depth = np.stack(
        [np.concatenate([cos, -sin], -1), np.concatenate([-sin, -cos], -1)], 1
    ).reshape(MZ * 2 * MT, 2 * PLANE)
    dhi, dlo = split_np(depth)
    depth_forward = np.concatenate([dhi, dlo], 0)
    depth_inverse = np.concatenate([dhi, dhi, dlo], 0)
    return forward, inverse, depth_forward, depth_inverse


def split(value):
    high = value.astype(BF16)
    return high, (value - high.astype(F32)).astype(BF16)


def dot(a, b):
    return lax.dot_general(a, b, (((1,), (0,)), ((), ())), preferred_element_type=F32)


def forward_transform(src, fwd, depth, zhi, zlo, out, exact):
    channels = src.shape[0]
    half = fwd.shape[0] // 2

    def pair(g, carry):
        block = jnp.concatenate([src[2 * g], src[2 * g + 1]], -1)
        if exact:
            res = dot(fwd[...], block.astype(BF16))
            res = res[:half] + res[half:]
        else:
            high, low = split(block)
            res = dot(fwd[...], high)
            res = res[:half] + res[half:] + dot(fwd[:half], low)
        for k in range(2):
            part = res[:, k * PLANE : (k + 1) * PLANE]
            high, low = split(jnp.concatenate([part[:XY], part[XY:]], -1))
            zhi[2 * g + k] = high
            zlo[2 * g + k] = low
        return carry

    lax.fori_loop(0, channels // 2, pair, 0)
    rows = out.shape[0]
    contract = (((1,), (1,)), ((), ()))
    high = zhi[...].reshape(channels * XY, 2 * PLANE)
    low = zlo[...].reshape(channels * XY, 2 * PLANE)
    first = lax.dot_general(depth[...], high, contract, preferred_element_type=F32)
    second = lax.dot_general(depth[:rows], low, contract, preferred_element_type=F32)
    out[...] = first[:rows] + first[rows:] + second


def inverse_transform(modes, depth, inv, ghi, glo, dst):
    outputs = dst.shape[0]
    cells = inv.shape[0] // 2
    high, low = split(modes[...])
    stacked = jnp.concatenate([high, low, high], 0)
    lines = lax.dot_general(
        stacked, depth[...], (((0,), (0,)), ((), ())), preferred_element_type=F32
    )
    high, low = split(lines.reshape(outputs, XY, 2 * PLANE))
    ghi[:, :XY] = high[:, :, :PLANE]
    ghi[:, XY:] = high[:, :, PLANE:]
    glo[:, :XY] = low[:, :, :PLANE]
    glo[:, XY:] = low[:, :, PLANE:]

    def pair(g, carry):
        high = jnp.concatenate([ghi[2 * g], ghi[2 * g + 1]], -1)
        low = jnp.concatenate([glo[2 * g], glo[2 * g + 1]], -1)
        res = dot(inv[...], high)
        res = res[:cells] + res[cells:] + dot(inv[:cells], low)
        dst[2 * g] = res[:, :PLANE]
        dst[2 * g + 1] = res[:, PLANE:]
        return carry

    lax.fori_loop(0, outputs // 2, pair, 0)


def first_kernel(fields, fwd, depth, out, src, zhi, zlo):
    rows = fields.shape[1]

    def line(i, carry):
        at = pl.multiple_of(i * PLANE, PLANE)
        to = pl.multiple_of(i * rows, rows)
        src[:, pl.ds(to, rows), :] = fields[:, :, pl.ds(at, PLANE)].astype(F32)
        return carry

    lax.fori_loop(0, NY, line, 0)
    forward_transform(src, fwd, depth, zhi, zlo, out, True)


def middle_kernel(
    modes, fields, cot, mix, mix_back, bias, fwd, inv, depth, depth_inv,
    activated, local, out, work, ghi, glo, zhi, zlo,
):
    channels, rows, _ = fields.shape
    inverse_transform(modes, depth_inv, inv, ghi, glo, work)
    flat = channels * rows

    def line(i, carry):
        at = pl.multiple_of(i * 2 * PLANE, 2 * PLANE)
        block = fields[:, :, pl.ds(at, 2 * PLANE)].astype(F32)
        near = dot(mix[...], block.reshape(flat, 2 * PLANE).astype(BF16))
        ups = []
        for k in range(2):
            here = pl.multiple_of(at + k * PLANE, PLANE)
            to = pl.multiple_of((2 * i + k) * rows, rows)
            far = work[:, pl.ds(to, rows), :].reshape(flat, PLANE)
            pre = far + near[:, k * PLANE : (k + 1) * PLANE] + bias[...]
            phi = 0.5 * (1.0 + lax.erf(pre * (1.0 / math.sqrt(2.0))))
            slope = phi + pre * jnp.exp(-0.5 * pre * pre) * (1.0 / math.sqrt(2.0 * math.pi))
            act = (pre * phi).reshape(channels, rows, PLANE)
            activated[:, :, pl.ds(here, PLANE)] = act.astype(BF16)
            c = cot[:, :, pl.ds(here, PLANE)].astype(F32).reshape(flat, PLANE)
            up = c * slope
            work[:, pl.ds(to, rows), :] = up.reshape(channels, rows, PLANE)
            ups.append(up)
        high, low = split(jnp.concatenate(ups, -1))
        back = dot(mix_back[...], high) + dot(mix_back[...], low)
        local[:, :, pl.ds(at, 2 * PLANE)] = back.reshape(channels, rows, 2 * PLANE)
        return carry

    lax.fori_loop(0, NY // 2, line, 0)
    forward_transform(work, fwd, depth, zhi, zlo, out, False)


def last_kernel(modes, local, inv, depth_inv, out, work, ghi, glo):
    rows = local.shape[1]
    inverse_transform(modes, depth_inv, inv, ghi, glo, work)

    def line(i, carry):
        at = pl.multiple_of(i * PLANE, PLANE)
        to = pl.multiple_of(i * rows, rows)
        value = work[:, pl.ds(to, rows), :] + local[:, :, pl.ds(at, PLANE)]
        out[:, :, pl.ds(at, PLANE)] = value.astype(BF16)
        return carry

    lax.fori_loop(0, NY, line, 0)


def call(body, outs, scratch):
    return pl.pallas_call(
        body,
        out_shape=outs,
        scratch_shapes=scratch,
        compiler_params=pltpu.CompilerParams(vmem_limit_bytes=VMEM_LIMIT),
    )


def swap(value):
    half = value.shape[0] // 2
    return jnp.concatenate([value[half:], value[:half]], 0)


def exchange_kernel(n, ns, backward, scale_in, scale_out, *refs):
    if backward:
        (partial, weight, cos, sin, spec_in, modes, spec, spec_all, up_all,
         recv, tiled, mixed, gat, s_got, u_got,
         send_a, recv_a, send_b, recv_b, send_s, recv_s, send_u, recv_u) = refs
    else:
        (partial, weight, cos, sin, modes, spec,
         recv, tiled, mixed, gat, send_a, recv_a, send_b, recv_b) = refs
    channels, rows, lanes = weight.shape
    width = lanes // channels
    me = lax.axis_index("space")
    mine = lax.axis_index("sample")

    barrier = pltpu.get_barrier_semaphore()
    for k in range(1, n):
        pl.semaphore_signal(
            barrier, inc=1, device_id={"space": lax.rem(me + k, n)},
            device_id_type=pl.DeviceIdType.MESH,
        )
    if backward:
        for k in range(1, ns):
            pl.semaphore_signal(
                barrier, inc=1, device_id={"sample": lax.rem(mine + k, ns)},
                device_id_type=pl.DeviceIdType.MESH,
            )
    pl.semaphore_wait(barrier, n - 1 + (ns - 1 if backward else 0))

    def start(src, dst, send, got, k, axis, target):
        copy = pltpu.make_async_remote_copy(
            src_ref=src, dst_ref=dst.at[k], send_sem=send.at[k], recv_sem=got.at[k],
            device_id={axis: target}, device_id_type=pl.DeviceIdType.MESH,
        )
        copy.start()
        return copy

    first = []
    for k in range(1, n):
        target = lax.rem(me + k, n)
        first.append(start(partial.at[target], recv, send_a, recv_a, k, "space", target))
    side = []
    if backward:
        for k in range(1, ns):
            target = lax.rem(mine + k, ns)
            side.append(start(spec_in, s_got, send_s, recv_s, k, "sample", target))

    row = lax.broadcasted_iota(jnp.int32, (rows, lanes), 0)
    top = row < rows // 2
    total = None
    for k in range(n):
        source = lax.rem(me + n - k, n)
        if k:
            first[k - 1].wait()
        value = recv[k] if k else partial[me]
        c, s = cos[pl.ds(source, 1), :], sin[pl.ds(source, 1), :]
        turned = swap(value) * s
        term = value * c + jnp.where(top, turned, -turned)
        total = term if total is None else total + term
    total = total * scale_in
    spec[...] = total
    if backward:
        for k in range(1, ns):
            target = lax.rem(mine + k, ns)
            side.append(start(spec, u_got, send_u, recv_u, k, "sample", target))

    block = tiled.shape[2]
    for c in range(channels):
        piece = total[:, c * width : (c + 1) * width]
        tiled[c] = jnp.concatenate([piece] * (block // width), -1)
    for at in range(0, lanes, block):
        size = min(block, lanes - at)

        def add(c, carry, at=at, size=size):
            w, t = weight[c, :, at : at + size], tiled[c, :, :size]
            return carry[0] + w * t, carry[1] + w * swap(t)

        zero = jnp.zeros((rows, size), F32)
        a, b = lax.fori_loop(0, channels, add, (zero, zero))
        half = rows // 2
        if backward:
            real, imag = a[:half] + a[half:], b[:half] - b[half:]
        else:
            real, imag = a[:half] - a[half:], b[:half] + b[half:]
        mixed[:, at : at + size] = jnp.concatenate([real, imag], 0)

    second = []
    for k in range(1, n):
        target = lax.rem(me + k, n)
        second.append(start(mixed, gat, send_b, recv_b, k, "space", target))
    c, s = cos[pl.ds(me, 1), :] * scale_out, sin[pl.ds(me, 1), :] * scale_out
    signed_s = jnp.where(top, -s, s)
    for k in range(n):
        source = lax.rem(me + n - k, n)
        if k:
            second[k - 1].wait()
        value = gat[k] if k else mixed[...]
        modes[source] = value * c + swap(value) * signed_s
    if backward:
        for copy in side:
            copy.wait()
        spec_all[mine] = spec_in[...]
        up_all[mine] = spec[...]
        for k in range(1, ns):
            source = lax.rem(mine + ns - k, ns)
            spec_all[source] = s_got[k]
            up_all[source] = u_got[k]


def exchange(partial, weight, cos, sin, spec_in, n, ns, scale_in, scale_out):
    backward = spec_in is not None
    channels, rows, lanes = weight.shape
    width = lanes // channels
    block = width * 128 // math.gcd(width, 128)
    one = jax.ShapeDtypeStruct((rows, lanes), F32)
    many = jax.ShapeDtypeStruct((n, rows, lanes), F32)
    outs = [many, one]
    slot = pltpu.VMEM((n, rows, lanes), F32)
    scratch = [slot, pltpu.VMEM((channels, rows, block), F32), pltpu.VMEM((rows, lanes), F32), slot]
    sems = [pltpu.SemaphoreType.DMA((n,))] * 4
    args = [partial, weight, cos, sin]
    if backward:
        outs += [jax.ShapeDtypeStruct((ns, rows, lanes), F32)] * 2
        scratch += [pltpu.VMEM((ns, rows, lanes), F32)] * 2
        sems += [pltpu.SemaphoreType.DMA((ns,))] * 4
        args.append(spec_in)
    vmem = pl.BlockSpec(memory_space=pltpu.VMEM)
    return pl.pallas_call(
        functools.partial(exchange_kernel, n, ns, backward, scale_in, scale_out),
        out_shape=outs,
        in_specs=[vmem] * len(args),
        out_specs=[vmem] * len(outs),
        scratch_shapes=scratch + sems,
        compiler_params=pltpu.CompilerParams(
            vmem_limit_bytes=VMEM_LIMIT, collective_id=int(backward), has_side_effects=True
        ),
    )(*args)


def shards(fields, cotangent, spectral_weight, point_weight, point_bias):
    _, rows, channels, columns = fields.shape
    space = lax.axis_size("space")
    samples = lax.axis_size("sample")
    fwd, inv, depth, depth_inv = [jnp.asarray(t) for t in tables(rows, space)]
    owned = MT * MZ // space
    own_rows = 2 * owned
    all_rows = 2 * MT * MZ
    lanes = channels * XY
    cells = NY * rows
    field = jnp.transpose(fields[0], (1, 0, 2))
    cot = jnp.transpose(cotangent[0], (1, 0, 2))
    eye = jnp.eye(rows, dtype=BF16)
    flat = channels * rows
    mix_back = (point_weight[:, None, :, None] * eye[None, :, None, :]).reshape(flat, flat)
    mix = (point_weight.T[:, None, :, None] * eye[None, :, None, :]).reshape(flat, flat)
    bias = jnp.broadcast_to(point_bias[:, None, None], (channels, rows, PLANE)).reshape(flat, PLANE)

    freq = np.tile(signed(MX), MY * channels)
    angle = 2 * np.pi * (freq[None, :] * np.arange(space)[:, None] * rows % NX) / NX
    turn_cos = np.cos(angle).astype(np.float32)
    turn_sin = np.sin(angle).astype(np.float32)

    z_buf = pltpu.VMEM((channels, XY, 2 * PLANE), BF16)
    g_buf = pltpu.VMEM((channels, 2 * XY, PLANE), BF16)
    w_buf = pltpu.VMEM((channels, cells, PLANE), F32)
    part = jax.ShapeDtypeStruct((all_rows, lanes), F32)
    grid_bf = jax.ShapeDtypeStruct((channels, rows, columns), BF16)
    grid_f = jax.ShapeDtypeStruct((channels, rows, columns), F32)

    weights = spectral_weight.astype(F32).reshape(2, channels, channels, owned, XY)
    weight_up = jnp.transpose(weights, (1, 0, 3, 2, 4)).reshape(channels, own_rows, lanes)
    weight_back = jnp.transpose(weights, (2, 0, 3, 1, 4)).reshape(channels, own_rows, lanes)

    partial = call(first_kernel, part, [w_buf, z_buf, z_buf])(field, fwd, depth)
    split_part = lambda value: value.reshape(space, own_rows, lanes)
    modes, spec_in = exchange(
        split_part(partial), weight_up, turn_cos, turn_sin, None,
        space, samples, 1.0, 1.0 / VOLUME,
    )
    activated, local, partial_up = call(
        middle_kernel, (grid_bf, grid_f, part), [w_buf, g_buf, g_buf, z_buf, z_buf]
    )(modes.reshape(all_rows, lanes), field, cot, mix, mix_back, bias, fwd, inv, depth, depth_inv)
    modes_back, _, spec_all, up_all = exchange(
        split_part(partial_up), weight_back, turn_cos, turn_sin, spec_in,
        space, samples, 1.0 / VOLUME, 1.0,
    )
    grad_input = call(last_kernel, grid_bf, [w_buf, g_buf, g_buf])(
        modes_back.reshape(all_rows, lanes), local, inv, depth_inv
    )

    mine = lax.axis_index("sample")
    count = owned * XY // samples

    def own_block(value):
        value = value.reshape(samples, 2, owned, channels, XY)
        value = jnp.transpose(value, (0, 1, 3, 2, 4)).reshape(samples, 2, channels, owned * XY)
        return lax.dynamic_slice_in_dim(value, mine * count, count, 3)

    a, b = own_block(spec_all), own_block(up_all)
    a_r, a_i = a[:, 0, :, None], a[:, 1, :, None]
    b_r, b_i = b[:, 0, None], b[:, 1, None]
    grad_r = sum(a_r[s] * b_r[s] + a_i[s] * b_i[s] for s in range(samples))
    grad_i = sum(a_r[s] * b_i[s] - a_i[s] * b_r[s] for s in range(samples))
    grad_spectral = jnp.stack([grad_r, grad_i])
    back_to = lambda value: jnp.transpose(value, (1, 0, 2))[None]
    return back_to(activated), back_to(grad_input), grad_spectral


def solution(mesh):
    return jax.shard_map(
        shards,
        mesh=mesh,
        in_specs=(
            P("sample", "space", None, None),
            P("sample", "space", None, None),
            P(None, None, None, "space"),
            P(),
            P(),
        ),
        out_specs=(
            P("sample", "space", None, None),
            P("sample", "space", None, None),
            P(None, None, None, ("space", "sample")),
        ),
        check_vma=False,
    )
```

```python
import functools
import math

import jax
import jax.numpy as jnp
import numpy as np
from jax import lax
from jax.experimental import pallas as pl
from jax.experimental.pallas import tpu as pltpu
from jax.sharding import PartitionSpec as P

NX, NY, NZ, NT = 64, 64, 32, 4
MX, MY, MZ, MT = 12, 12, 8, 4
VOLUME = NX * NY * NZ * NT
PLANE = NZ * NT
XY = MX * MY
BF16, F32 = jnp.bfloat16, jnp.float32
VMEM_LIMIT = 60 * 1024 * 1024


def signed(modes):
    index = np.arange(modes)
    return np.where(index < modes // 2, index, index - modes)


def split_np(table):
    high = table.astype(np.float32).astype(BF16)
    low = (table - high.astype(np.float64)).astype(np.float32).astype(BF16)
    return high, low


def tables(rows, space):
    y, x = np.arange(NY)[:, None], np.arange(rows)[None, :]
    fy, fx = signed(MY)[:, None], signed(MX)[None, :]
    phi = 2 * np.pi * (
        fy.reshape(MY, 1, 1, 1) * y.reshape(1, 1, NY, 1) / NY
        + fx.reshape(1, MX, 1, 1) * x.reshape(1, 1, 1, rows) / NX
    ).reshape(XY, NY * rows)
    plane = np.concatenate([np.cos(phi), np.sin(phi)], 0)
    hi, lo = split_np(plane)
    forward = np.concatenate([hi, lo], 0)
    inverse = np.concatenate([hi.T, lo.T], 0)
    fz, ft = signed(MZ), signed(MT)
    z, t = np.arange(NZ), np.arange(NT)
    psi = 2 * np.pi * (
        fz.reshape(MZ, 1, 1, 1) * z.reshape(1, 1, NZ, 1) / NZ
        + ft.reshape(1, MT, 1, 1) * t.reshape(1, 1, 1, NT) / NT
    ).reshape(space, MZ * MT // space, PLANE)
    cos, sin = np.cos(psi), np.sin(psi)
    depth = np.stack(
        [np.concatenate([cos, -sin], -1), np.concatenate([-sin, -cos], -1)], 1
    ).reshape(MZ * 2 * MT, 2 * PLANE)
    dhi, dlo = split_np(depth)
    depth_forward = np.concatenate([dhi, dlo], 0)
    depth_inverse = np.concatenate([dhi, dhi, dlo], 0)
    return forward, inverse, depth_forward, depth_inverse


def split(value):
    high = value.astype(BF16)
    return high, (value - high.astype(F32)).astype(BF16)


def dot(a, b):
    return lax.dot_general(a, b, (((1,), (0,)), ((), ())), preferred_element_type=F32)


def forward_transform(src, fwd, depth, zhi, zlo, out, exact):
    channels = src.shape[0]
    half = fwd.shape[0] // 2

    def pair(g, carry):
        block = jnp.concatenate([src[2 * g], src[2 * g + 1]], -1)
        if exact:
            res = dot(fwd[...], block.astype(BF16))
            res = res[:half] + res[half:]
        else:
            high, low = split(block)
            res = dot(fwd[...], high)
            res = res[:half] + res[half:] + dot(fwd[:half], low)
        for k in range(2):
            part = res[:, k * PLANE : (k + 1) * PLANE]
            high, low = split(jnp.concatenate([part[:XY], part[XY:]], -1))
            zhi[2 * g + k] = high
            zlo[2 * g + k] = low
        return carry

    lax.fori_loop(0, channels // 2, pair, 0)
    rows = out.shape[0]
    contract = (((1,), (1,)), ((), ()))
    high = zhi[...].reshape(channels * XY, 2 * PLANE)
    low = zlo[...].reshape(channels * XY, 2 * PLANE)
    first = lax.dot_general(depth[...], high, contract, preferred_element_type=F32)
    second = lax.dot_general(depth[:rows], low, contract, preferred_element_type=F32)
    out[...] = first[:rows] + first[rows:] + second


def inverse_transform(modes, depth, inv, ghi, glo, dst):
    outputs = dst.shape[0]
    cells = inv.shape[0] // 2
    high, low = split(modes[...])
    stacked = jnp.concatenate([high, low, high], 0)
    lines = lax.dot_general(
        stacked, depth[...], (((0,), (0,)), ((), ())), preferred_element_type=F32
    )
    high, low = split(lines.reshape(outputs, XY, 2 * PLANE))
    ghi[:, :XY] = high[:, :, :PLANE]
    ghi[:, XY:] = high[:, :, PLANE:]
    glo[:, :XY] = low[:, :, :PLANE]
    glo[:, XY:] = low[:, :, PLANE:]

    def pair(g, carry):
        high = jnp.concatenate([ghi[2 * g], ghi[2 * g + 1]], -1)
        low = jnp.concatenate([glo[2 * g], glo[2 * g + 1]], -1)
        res = dot(inv[...], high)
        res = res[:cells] + res[cells:] + dot(inv[:cells], low)
        dst[2 * g] = res[:, :PLANE]
        dst[2 * g + 1] = res[:, PLANE:]
        return carry

    lax.fori_loop(0, outputs // 2, pair, 0)


def first_kernel(fields, fwd, depth, out, src, zhi, zlo):
    rows = fields.shape[1]

    def line(i, carry):
        at = pl.multiple_of(i * PLANE, PLANE)
        to = pl.multiple_of(i * rows, rows)
        src[:, pl.ds(to, rows), :] = fields[:, :, pl.ds(at, PLANE)].astype(F32)
        return carry

    lax.fori_loop(0, NY, line, 0)
    forward_transform(src, fwd, depth, zhi, zlo, out, True)


def middle_kernel(
    modes, fields, cot, point, point_t, bias_row, copies, copies_t, same, fwd, inv, depth, depth_inv,
    activated, local, out, work, ghi, glo, zhi, zlo, mix, mix_back, bias,
):
    channels, rows, _ = fields.shape
    inverse_transform(modes, depth_inv, inv, ghi, glo, work)
    flat = channels * rows

    def spread(matrix):
        half = dot(copies[...], matrix).astype(BF16)
        return dot(half, copies_t[...]).astype(BF16) * same[...]

    mix_back[...] = spread(point[...])
    mix[...] = spread(point_t[...])
    column = jnp.sum(copies[...].astype(F32) * bias_row[...], -1, keepdims=True)
    bias[...] = jnp.broadcast_to(column, (flat, PLANE))

    def line(i, carry):
        at = pl.multiple_of(i * 2 * PLANE, 2 * PLANE)
        block = fields[:, :, pl.ds(at, 2 * PLANE)].astype(F32)
        near = dot(mix[...], block.reshape(flat, 2 * PLANE).astype(BF16))
        ups = []
        for k in range(2):
            here = pl.multiple_of(at + k * PLANE, PLANE)
            to = pl.multiple_of((2 * i + k) * rows, rows)
            far = work[:, pl.ds(to, rows), :].reshape(flat, PLANE)
            pre = far + near[:, k * PLANE : (k + 1) * PLANE] + bias[...]
            phi = 0.5 * (1.0 + lax.erf(pre * (1.0 / math.sqrt(2.0))))
            slope = phi + pre * jnp.exp(-0.5 * pre * pre) * (1.0 / math.sqrt(2.0 * math.pi))
            act = (pre * phi).reshape(channels, rows, PLANE)
            activated[:, :, pl.ds(here, PLANE)] = act.astype(BF16)
            c = cot[:, :, pl.ds(here, PLANE)].astype(F32).reshape(flat, PLANE)
            up = c * slope
            work[:, pl.ds(to, rows), :] = up.reshape(channels, rows, PLANE)
            ups.append(up)
        high, low = split(jnp.concatenate(ups, -1))
        back = dot(mix_back[...], high) + dot(mix_back[...], low)
        local[:, :, pl.ds(at, 2 * PLANE)] = back.reshape(channels, rows, 2 * PLANE)
        return carry

    lax.fori_loop(0, NY // 2, line, 0)
    forward_transform(work, fwd, depth, zhi, zlo, out, False)


def last_kernel(modes, local, spec_all, up_all, inv, depth_inv, out, grad, work, ghi, glo):
    rows = local.shape[1]
    samples, _, channels, count = spec_all.shape
    inverse_transform(modes, depth_inv, inv, ghi, glo, work)

    def line(i, carry):
        at = pl.multiple_of(i * PLANE, PLANE)
        to = pl.multiple_of(i * rows, rows)
        value = work[:, pl.ds(to, rows), :] + local[:, :, pl.ds(at, PLANE)]
        out[:, :, pl.ds(at, PLANE)] = value.astype(BF16)
        return carry

    lax.fori_loop(0, NY, line, 0)

    def term(c, carry):
        real = jnp.zeros((channels, count), F32)
        imag = jnp.zeros((channels, count), F32)
        for s in range(samples):
            a_r, a_i = spec_all[s, 0, pl.ds(c, 1), :], spec_all[s, 1, pl.ds(c, 1), :]
            b_r, b_i = up_all[s, 0], up_all[s, 1]
            real = real + (a_r * b_r + a_i * b_i)
            imag = imag + (a_r * b_i - a_i * b_r)
        grad[c, :, 0, :] = real
        grad[c, :, 1, :] = imag
        return carry

    lax.fori_loop(0, channels, term, 0)


def call(body, outs, scratch):
    return pl.pallas_call(
        body,
        out_shape=outs,
        scratch_shapes=scratch,
        compiler_params=pltpu.CompilerParams(vmem_limit_bytes=VMEM_LIMIT),
    )


def swap(value):
    half = value.shape[0] // 2
    return jnp.concatenate([value[half:], value[:half]], 0)


def exchange_kernel(n, ns, backward, scale_in, scale_out, *refs):
    if backward:
        (partial, weight, cos, sin, spec_in, modes, spec_all, up_all,
         recv, stage, lined, out_lined, mixed, gat, s_got, u_got, spec,
         send_a, recv_a, send_b, recv_b, send_s, recv_s, send_u, recv_u) = refs
    else:
        (partial, weight, cos, sin, modes, spec,
         recv, stage, lined, out_lined, mixed, gat, send_a, recv_a, send_b, recv_b) = refs
    _, rows, lanes = partial.shape
    channels, width = stage.shape[0], stage.shape[2]
    owned = rows // 2
    per = ns // owned
    count = width // per
    me = lax.axis_index("space")
    mine = lax.axis_index("sample")

    barrier = pltpu.get_barrier_semaphore()
    for k in range(1, n):
        pl.semaphore_signal(
            barrier, inc=1, device_id={"space": lax.rem(me + k, n)},
            device_id_type=pl.DeviceIdType.MESH,
        )
    if backward:
        for k in range(1, ns):
            pl.semaphore_signal(
                barrier, inc=1, device_id={"sample": lax.rem(mine + k, ns)},
                device_id_type=pl.DeviceIdType.MESH,
            )
    pl.semaphore_wait(barrier, n - 1 + (ns - 1 if backward else 0))

    def start(src, dst, send, got, k, axis, target):
        copy = pltpu.make_async_remote_copy(
            src_ref=src, dst_ref=dst.at[k], send_sem=send.at[k], recv_sem=got.at[k],
            device_id={axis: target}, device_id_type=pl.DeviceIdType.MESH,
        )
        copy.start()
        return copy

    first = []
    for k in range(1, n):
        target = lax.rem(me + k, n)
        first.append(start(partial.at[target], recv, send_a, recv_a, k, "space", target))
    side = []
    if backward:
        for k in range(1, ns):
            target = lax.rem(mine + k, ns)
            side.append(start(spec_in.at[target], s_got, send_s, recv_s, k, "sample", target))

    row = lax.broadcasted_iota(jnp.int32, (rows, lanes), 0)
    top = row < rows // 2
    total = None
    for k in range(n):
        source = lax.rem(me + n - k, n)
        if k:
            first[k - 1].wait()
        value = recv[k] if k else partial[me]
        c, s = cos[pl.ds(source, 1), :], sin[pl.ds(source, 1), :]
        turned = swap(value) * s
        term = value * c + jnp.where(top, turned, -turned)
        total = term if total is None else total + term
    total = total * scale_in
    for c in range(channels):
        stage[c] = total[:, c * width : (c + 1) * width]
    for j in range(rows):
        r, q = j // owned, j % owned
        block = stage[:, j, :]
        lined[r, :, q * width : (q + 1) * width] = block
        for p in range(per):
            spec[q * per + p, r] = block[:, p * count : (p + 1) * count]
    if backward:
        for k in range(1, ns):
            target = lax.rem(mine + k, ns)
            side.append(start(spec.at[target], u_got, send_u, recv_u, k, "sample", target))

    if backward:

        def reduce(c, carry):
            w_r, w_i = weight[0, c], weight[1, c]
            u_r, u_i = lined[0], lined[1]
            out_lined[0, pl.ds(c, 1), :] = jnp.sum(w_r * u_r + w_i * u_i, 0, keepdims=True)
            out_lined[1, pl.ds(c, 1), :] = jnp.sum(w_r * u_i - w_i * u_r, 0, keepdims=True)
            return carry

        lax.fori_loop(0, channels, reduce, 0)
    else:

        def add(c, carry):
            w_r, w_i = weight[0, c], weight[1, c]
            s_r, s_i = lined[0, pl.ds(c, 1), :], lined[1, pl.ds(c, 1), :]
            return carry[0] + (w_r * s_r - w_i * s_i), carry[1] + (w_r * s_i + w_i * s_r)

        zero = jnp.zeros((channels, owned * width), F32)
        real, imag = lax.fori_loop(0, channels, add, (zero, zero))
        out_lined[0] = real
        out_lined[1] = imag
    for j in range(rows):
        r, q = j // owned, j % owned
        stage[:, j, :] = out_lined[r, :, q * width : (q + 1) * width]
    for c in range(channels):
        mixed[:, c * width : (c + 1) * width] = stage[c]

    second = []
    for k in range(1, n):
        target = lax.rem(me + k, n)
        second.append(start(mixed, gat, send_b, recv_b, k, "space", target))
    c, s = cos[pl.ds(me, 1), :] * scale_out, sin[pl.ds(me, 1), :] * scale_out
    signed_s = jnp.where(top, -s, s)
    for k in range(n):
        source = lax.rem(me + n - k, n)
        if k:
            second[k - 1].wait()
        value = gat[k] if k else mixed[...]
        modes[source] = value * c + swap(value) * signed_s
    if backward:
        for copy in side:
            copy.wait()
        spec_all[0] = spec_in[mine]
        up_all[0] = spec[mine]
        for k in range(1, ns):
            spec_all[k] = s_got[k]
            up_all[k] = u_got[k]


def exchange(partial, weight, cos, sin, spec_in, n, ns, scale_in, scale_out):
    backward = spec_in is not None
    _, channels, _, modes = weight.shape
    _, rows, lanes = partial.shape
    many = jax.ShapeDtypeStruct((n, rows, lanes), F32)
    kept = (ns, 2, channels, modes // ns)
    outs = [many] if backward else [many, jax.ShapeDtypeStruct(kept, F32)]
    slot = pltpu.VMEM((n, rows, lanes), F32)
    line = pltpu.VMEM((2, channels, modes), F32)
    stage = pltpu.VMEM((channels, rows, lanes // channels), F32)
    scratch = [slot, stage, line, line, pltpu.VMEM((rows, lanes), F32), slot]
    sems = [pltpu.SemaphoreType.DMA((n,))] * 4
    args = [partial, weight, cos, sin]
    if backward:
        outs += [jax.ShapeDtypeStruct(kept, F32)] * 2
        scratch += [pltpu.VMEM(kept, F32)] * 3
        sems += [pltpu.SemaphoreType.DMA((ns,))] * 4
        args.append(spec_in)
    vmem = pl.BlockSpec(memory_space=pltpu.VMEM)
    return pl.pallas_call(
        functools.partial(exchange_kernel, n, ns, backward, scale_in, scale_out),
        out_shape=outs,
        in_specs=[vmem] * len(args),
        out_specs=[vmem] * len(outs),
        scratch_shapes=scratch + sems,
        compiler_params=pltpu.CompilerParams(
            vmem_limit_bytes=VMEM_LIMIT, collective_id=int(backward), has_side_effects=True
        ),
    )(*args)


def shards(fields, cotangent, spectral_weight, point_weight, point_bias):
    _, rows, channels, columns = fields.shape
    space = lax.axis_size("space")
    samples = lax.axis_size("sample")
    fwd, inv, depth, depth_inv = [jnp.asarray(t) for t in tables(rows, space)]
    owned = MT * MZ // space
    own_rows = 2 * owned
    all_rows = 2 * MT * MZ
    lanes = channels * XY
    cells = NY * rows
    field = jnp.transpose(fields[0], (1, 0, 2))
    cot = jnp.transpose(cotangent[0], (1, 0, 2))
    flat = channels * rows
    copies = np.repeat(np.eye(channels), rows, 0).astype(BF16)
    same = np.tile(np.eye(rows), (channels, channels)).astype(BF16)
    flat_buf = pltpu.VMEM((flat, flat), BF16)

    freq = np.tile(signed(MX), MY * channels)
    angle = 2 * np.pi * (freq[None, :] * np.arange(space)[:, None] * rows % NX) / NX
    turn_cos = np.cos(angle).astype(np.float32)
    turn_sin = np.sin(angle).astype(np.float32)

    z_buf = pltpu.VMEM((channels, XY, 2 * PLANE), BF16)
    g_buf = pltpu.VMEM((channels, 2 * XY, PLANE), BF16)
    w_buf = pltpu.VMEM((channels, cells, PLANE), F32)
    part = jax.ShapeDtypeStruct((all_rows, lanes), F32)
    grid_bf = jax.ShapeDtypeStruct((channels, rows, columns), BF16)
    grid_f = jax.ShapeDtypeStruct((channels, rows, columns), F32)

    weights = spectral_weight.astype(F32)

    partial = call(first_kernel, part, [w_buf, z_buf, z_buf])(field, fwd, depth)
    split_part = lambda value: value.reshape(space, own_rows, lanes)
    modes, spec_in = exchange(
        split_part(partial), weights, turn_cos, turn_sin, None,
        space, samples, 1.0, 1.0 / VOLUME,
    )
    activated, local, partial_up = call(
        middle_kernel, (grid_bf, grid_f, part), [w_buf, g_buf, g_buf, z_buf, z_buf, flat_buf, flat_buf, pltpu.VMEM((flat, PLANE), F32)]
    )(
        modes.reshape(all_rows, lanes), field, cot, point_weight, point_weight.T,
        point_bias[None], copies, copies.T, same, fwd, inv, depth, depth_inv,
    )
    modes_back, spec_all, up_all = exchange(
        split_part(partial_up), weights, turn_cos, turn_sin, spec_in,
        space, samples, 1.0 / VOLUME, 1.0,
    )
    count = owned * XY // samples
    grad_shape = jax.ShapeDtypeStruct((channels, channels, 2, count), F32)
    grad_input, grad = call(last_kernel, (grid_bf, grad_shape), [w_buf, g_buf, g_buf])(
        modes_back.reshape(all_rows, lanes), local, spec_all, up_all, inv, depth_inv
    )
    grad_spectral = jnp.transpose(grad, (2, 0, 1, 3))
    back_to = lambda value: jnp.transpose(value, (1, 0, 2))[None]
    return back_to(activated), back_to(grad_input), grad_spectral


def solution(mesh):
    return jax.shard_map(
        shards,
        mesh=mesh,
        in_specs=(
            P("sample", "space", None, None),
            P("sample", "space", None, None),
            P(None, None, None, "space"),
            P(),
            P(),
        ),
        out_specs=(
            P("sample", "space", None, None),
            P("sample", "space", None, None),
            P(None, None, None, ("space", "sample")),
        ),
        check_vma=False,
    )
```

```python
import functools
import math

import jax
import jax.numpy as jnp
import numpy as np
from jax import lax
from jax.experimental import pallas as pl
from jax.experimental.pallas import tpu as pltpu
from jax.sharding import PartitionSpec as P

NX, NY, NZ, NT = 64, 64, 32, 4
MX, MY, MZ, MT = 12, 12, 8, 4
VOLUME = NX * NY * NZ * NT
PLANE = NZ * NT
XY = MX * MY
BF16, F32 = jnp.bfloat16, jnp.float32
VMEM_LIMIT = 60 * 1024 * 1024


def signed(modes):
    index = np.arange(modes)
    return np.where(index < modes // 2, index, index - modes)


def split_np(table):
    high = table.astype(np.float32).astype(BF16)
    low = (table - high.astype(np.float64)).astype(np.float32).astype(BF16)
    return high, low


def tables(rows, space):
    y, x = np.arange(NY)[:, None], np.arange(rows)[None, :]
    fy, fx = signed(MY)[:, None], signed(MX)[None, :]
    phi = 2 * np.pi * (
        fy.reshape(MY, 1, 1, 1) * y.reshape(1, 1, NY, 1) / NY
        + fx.reshape(1, MX, 1, 1) * x.reshape(1, 1, 1, rows) / NX
    ).reshape(XY, NY * rows)
    plane = np.concatenate([np.cos(phi), np.sin(phi)], 0)
    hi, lo = split_np(plane)
    forward = np.concatenate([hi, lo], 0)
    inverse = np.concatenate([hi.T, lo.T], 0)
    fz, ft = signed(MZ), signed(MT)
    z, t = np.arange(NZ), np.arange(NT)
    psi = 2 * np.pi * (
        fz.reshape(MZ, 1, 1, 1) * z.reshape(1, 1, NZ, 1) / NZ
        + ft.reshape(1, MT, 1, 1) * t.reshape(1, 1, 1, NT) / NT
    ).reshape(space, MZ * MT // space, PLANE)
    cos, sin = np.cos(psi), np.sin(psi)
    depth = np.stack(
        [np.concatenate([cos, -sin], -1), np.concatenate([-sin, -cos], -1)], 1
    ).reshape(MZ * 2 * MT, 2 * PLANE)
    dhi, dlo = split_np(depth)
    depth_forward = np.concatenate([dhi, dlo], 0)
    depth_inverse = np.concatenate([dhi, dhi, dlo], 0)
    return forward, inverse, depth_forward, depth_inverse


def split(value):
    high = value.astype(BF16)
    return high, (value - high.astype(F32)).astype(BF16)


def dot(a, b):
    return lax.dot_general(a, b, (((1,), (0,)), ((), ())), preferred_element_type=F32)


def forward_transform(src, fwd, depth, zhi, zlo, out, exact):
    channels = src.shape[0]
    half = fwd.shape[0] // 2

    def pair(g, carry):
        block = jnp.concatenate([src[2 * g], src[2 * g + 1]], -1)
        if exact:
            res = dot(fwd[...], block.astype(BF16))
            res = res[:half] + res[half:]
        else:
            high, low = split(block)
            res = dot(fwd[...], high)
            res = res[:half] + res[half:] + dot(fwd[:half], low)
        for k in range(2):
            part = res[:, k * PLANE : (k + 1) * PLANE]
            high, low = split(jnp.concatenate([part[:XY], part[XY:]], -1))
            zhi[2 * g + k] = high
            zlo[2 * g + k] = low
        return carry

    lax.fori_loop(0, channels // 2, pair, 0)
    rows = out.shape[0]
    contract = (((1,), (1,)), ((), ()))
    high = zhi[...].reshape(channels * XY, 2 * PLANE)
    low = zlo[...].reshape(channels * XY, 2 * PLANE)
    first = lax.dot_general(depth[...], high, contract, preferred_element_type=F32)
    second = lax.dot_general(depth[:rows], low, contract, preferred_element_type=F32)
    out[...] = first[:rows] + first[rows:] + second


def inverse_transform(modes, depth, inv, ghi, glo, dst):
    outputs = dst.shape[0]
    cells = inv.shape[0] // 2
    high, low = split(modes[...])
    stacked = jnp.concatenate([high, low, high], 0)
    lines = lax.dot_general(
        stacked, depth[...], (((0,), (0,)), ((), ())), preferred_element_type=F32
    )
    high, low = split(lines.reshape(outputs, XY, 2 * PLANE))
    ghi[:, :XY] = high[:, :, :PLANE]
    ghi[:, XY:] = high[:, :, PLANE:]
    glo[:, :XY] = low[:, :, :PLANE]
    glo[:, XY:] = low[:, :, PLANE:]

    def pair(g, carry):
        high = jnp.concatenate([ghi[2 * g], ghi[2 * g + 1]], -1)
        low = jnp.concatenate([glo[2 * g], glo[2 * g + 1]], -1)
        res = dot(inv[...], high)
        res = res[:cells] + res[cells:] + dot(inv[:cells], low)
        dst[2 * g] = res[:, :PLANE]
        dst[2 * g + 1] = res[:, PLANE:]
        return carry

    lax.fori_loop(0, outputs // 2, pair, 0)


def first_kernel(fields, fwd, depth, out, src, zhi, zlo):
    rows = fields.shape[1]

    def line(i, carry):
        at = pl.multiple_of(i * PLANE, PLANE)
        to = pl.multiple_of(i * rows, rows)
        src[:, pl.ds(to, rows), :] = fields[:, :, pl.ds(at, PLANE)].astype(F32)
        return carry

    lax.fori_loop(0, NY, line, 0)
    forward_transform(src, fwd, depth, zhi, zlo, out, True)


def middle_kernel(
    modes, fields, cot, point, point_t, bias_row, copies, copies_t, same, fwd, inv, depth, depth_inv,
    activated, local, out, work, ghi, glo, zhi, zlo, mix, mix_back, bias,
):
    channels, rows, _ = fields.shape
    inverse_transform(modes, depth_inv, inv, ghi, glo, work)
    flat = channels * rows

    def spread(matrix):
        half = dot(copies[...], matrix).astype(BF16)
        return dot(half, copies_t[...]).astype(BF16) * same[...]

    mix_back[...] = spread(point[...])
    mix[...] = spread(point_t[...])
    column = jnp.sum(copies[...].astype(F32) * bias_row[...], -1, keepdims=True)
    bias[...] = jnp.broadcast_to(column, (flat, PLANE))

    def line(i, carry):
        at = pl.multiple_of(i * 2 * PLANE, 2 * PLANE)
        block = fields[:, :, pl.ds(at, 2 * PLANE)].astype(F32)
        near = dot(mix[...], block.reshape(flat, 2 * PLANE).astype(BF16))
        ups = []
        for k in range(2):
            here = pl.multiple_of(at + k * PLANE, PLANE)
            to = pl.multiple_of((2 * i + k) * rows, rows)
            far = work[:, pl.ds(to, rows), :].reshape(flat, PLANE)
            pre = far + near[:, k * PLANE : (k + 1) * PLANE] + bias[...]
            phi = 0.5 * (1.0 + lax.erf(pre * (1.0 / math.sqrt(2.0))))
            slope = phi + pre * jnp.exp(-0.5 * pre * pre) * (1.0 / math.sqrt(2.0 * math.pi))
            act = (pre * phi).reshape(channels, rows, PLANE)
            activated[:, :, pl.ds(here, PLANE)] = act.astype(BF16)
            c = cot[:, :, pl.ds(here, PLANE)].astype(F32).reshape(flat, PLANE)
            up = c * slope
            work[:, pl.ds(to, rows), :] = up.reshape(channels, rows, PLANE)
            ups.append(up)
        high, low = split(jnp.concatenate(ups, -1))
        back = dot(mix_back[...], high) + dot(mix_back[...], low)
        local[:, :, pl.ds(at, 2 * PLANE)] = back.reshape(channels, rows, 2 * PLANE)
        return carry

    lax.fori_loop(0, NY // 2, line, 0)
    forward_transform(work, fwd, depth, zhi, zlo, out, False)


def last_kernel(modes, local, spec_all, up_all, inv, depth_inv, out, grad, work, ghi, glo):
    rows = local.shape[1]
    samples, _, channels, count = spec_all.shape
    inverse_transform(modes, depth_inv, inv, ghi, glo, work)

    def line(i, carry):
        at = pl.multiple_of(i * PLANE, PLANE)
        to = pl.multiple_of(i * rows, rows)
        value = work[:, pl.ds(to, rows), :] + local[:, :, pl.ds(at, PLANE)]
        out[:, :, pl.ds(at, PLANE)] = value.astype(BF16)
        return carry

    lax.fori_loop(0, NY, line, 0)

    def term(c, carry):
        real = jnp.zeros((channels, count), F32)
        imag = jnp.zeros((channels, count), F32)
        for s in range(samples):
            a_r, a_i = spec_all[s, 0, pl.ds(c, 1), :], spec_all[s, 1, pl.ds(c, 1), :]
            b_r, b_i = up_all[s, 0], up_all[s, 1]
            real = real + (a_r * b_r + a_i * b_i)
            imag = imag + (a_r * b_i - a_i * b_r)
        grad[c, :, 0, :] = real
        grad[c, :, 1, :] = imag
        return carry

    lax.fori_loop(0, channels, term, 0)


def call(body, outs, scratch):
    return pl.pallas_call(
        body,
        out_shape=outs,
        scratch_shapes=scratch,
        compiler_params=pltpu.CompilerParams(vmem_limit_bytes=VMEM_LIMIT),
    )


def swap(value):
    half = value.shape[0] // 2
    return jnp.concatenate([value[half:], value[:half]], 0)


def exchange_kernel(n, ns, backward, scale_in, scale_out, *refs):
    if backward:
        (partial, weight, cos, sin, spec_in, modes, spec_all, up_all,
         recv, stage, lined, out_lined, mixed, gat, pre, joined, gat_near, s_got, u_got, spec,
         send_a, recv_a, send_b, recv_b, send_c, recv_c, send_d, recv_d, send_s, recv_s, send_u, recv_u) = refs
    else:
        (partial, weight, cos, sin, modes, spec,
         recv, stage, lined, out_lined, mixed, gat, pre, joined, gat_near, send_a, recv_a, send_b, recv_b, send_c, recv_c, send_d, recv_d) = refs
    _, rows, lanes = partial.shape
    channels, width = stage.shape[0], stage.shape[2]
    owned = rows // 2
    per = ns // owned
    count = width // per
    me = lax.axis_index("space")
    mine = lax.axis_index("sample")

    barrier = pltpu.get_barrier_semaphore()
    for k in range(1, n):
        pl.semaphore_signal(
            barrier, inc=1, device_id={"space": lax.rem(me + k, n)},
            device_id_type=pl.DeviceIdType.MESH,
        )
    if backward:
        for k in range(1, ns):
            pl.semaphore_signal(
                barrier, inc=1, device_id={"sample": lax.rem(mine + k, ns)},
                device_id_type=pl.DeviceIdType.MESH,
            )
    pl.semaphore_wait(barrier, n - 1 + (ns - 1 if backward else 0))

    def start(src, dst, send, got, k, axis, target):
        copy = pltpu.make_async_remote_copy(
            src_ref=src, dst_ref=dst.at[k], send_sem=send.at[k], recv_sem=got.at[k],
            device_id={axis: target}, device_id_type=pl.DeviceIdType.MESH,
        )
        copy.start()
        return copy

    sibling = me + 1 - 2 * lax.rem(me, 2)
    near = {}
    for k in range(0, n, 2):
        target = lax.rem(sibling + k, n)
        near[k] = start(partial.at[target], pre, send_d, recv_d, k, "space", sibling)
    side = []
    if backward:
        for k in range(1, ns):
            target = lax.rem(mine + k, ns)
            side.append(start(spec_in.at[target], s_got, send_s, recv_s, k, "sample", target))

    row = lax.broadcasted_iota(jnp.int32, (rows, lanes), 0)
    top = row < rows // 2

    def turn(value, source):
        c, s = cos[pl.ds(source, 1), :], sin[pl.ds(source, 1), :]
        turned = swap(value) * s
        return value * c + jnp.where(top, turned, -turned)

    first = {}
    for k in list(range(2, n, 2)) + [0]:
        near[k].wait()
        target = lax.rem(me + k, n)
        joined[k] = turn(partial[target], me) + turn(pre[k], sibling)
        if k:
            first[k] = start(joined.at[k], recv, send_a, recv_a, k, "space", target)
    total = joined[0]
    for k in range(2, n, 2):
        first[k].wait()
        total = total + recv[k]
    total = total * scale_in
    for c in range(channels):
        stage[c] = total[:, c * width : (c + 1) * width]
    for j in range(rows):
        r, q = j // owned, j % owned
        block = stage[:, j, :]
        lined[r, :, q * width : (q + 1) * width] = block
        for p in range(per):
            spec[q * per + p, r] = block[:, p * count : (p + 1) * count]
    if backward:
        for k in range(1, ns):
            target = lax.rem(mine + k, ns)
            side.append(start(spec.at[target], u_got, send_u, recv_u, k, "sample", target))

    if backward:

        def reduce(c, carry):
            w_r, w_i = weight[0, c], weight[1, c]
            u_r, u_i = lined[0], lined[1]
            out_lined[0, pl.ds(c, 1), :] = jnp.sum(w_r * u_r + w_i * u_i, 0, keepdims=True)
            out_lined[1, pl.ds(c, 1), :] = jnp.sum(w_r * u_i - w_i * u_r, 0, keepdims=True)
            return carry

        lax.fori_loop(0, channels, reduce, 0)
    else:

        def add(c, carry):
            w_r, w_i = weight[0, c], weight[1, c]
            s_r, s_i = lined[0, pl.ds(c, 1), :], lined[1, pl.ds(c, 1), :]
            return carry[0] + (w_r * s_r - w_i * s_i), carry[1] + (w_r * s_i + w_i * s_r)

        zero = jnp.zeros((channels, owned * width), F32)
        real, imag = lax.fori_loop(0, channels, add, (zero, zero))
        out_lined[0] = real
        out_lined[1] = imag
    for j in range(rows):
        r, q = j // owned, j % owned
        stage[:, j, :] = out_lined[r, :, q * width : (q + 1) * width]
    for c in range(channels):
        mixed[:, c * width : (c + 1) * width] = stage[c]

    second, relay = {}, {}
    for k in range(2, n, 2):
        second[k] = start(mixed, gat, send_b, recv_b, k, "space", lax.rem(me + k, n))
    relay[0] = start(mixed, gat_near, send_c, recv_c, 0, "space", sibling)
    c, s = cos[pl.ds(me, 1), :] * scale_out, sin[pl.ds(me, 1), :] * scale_out
    signed_s = jnp.where(top, -s, s)

    def place(value, source):
        modes[source] = value * c + swap(value) * signed_s

    place(mixed[...], me)
    for k in range(2, n, 2):
        second[k].wait()
        relay[k] = start(gat.at[k], gat_near, send_c, recv_c, k, "space", sibling)
        place(gat[k], lax.rem(me + n - k, n))
    for k in range(0, n, 2):
        relay[k].wait()
        place(gat_near[k], lax.rem(sibling + n - k, n))
    if backward:
        for copy in side:
            copy.wait()
        spec_all[0] = spec_in[mine]
        up_all[0] = spec[mine]
        for k in range(1, ns):
            spec_all[k] = s_got[k]
            up_all[k] = u_got[k]


def exchange(partial, weight, cos, sin, spec_in, n, ns, scale_in, scale_out):
    backward = spec_in is not None
    _, channels, _, modes = weight.shape
    _, rows, lanes = partial.shape
    many = jax.ShapeDtypeStruct((n, rows, lanes), F32)
    kept = (ns, 2, channels, modes // ns)
    outs = [many] if backward else [many, jax.ShapeDtypeStruct(kept, F32)]
    slot = pltpu.VMEM((n, rows, lanes), F32)
    line = pltpu.VMEM((2, channels, modes), F32)
    stage = pltpu.VMEM((channels, rows, lanes // channels), F32)
    scratch = [slot, stage, line, line, pltpu.VMEM((rows, lanes), F32), slot, slot, slot, slot]
    sems = [pltpu.SemaphoreType.DMA((n,))] * 8
    args = [partial, weight, cos, sin]
    if backward:
        outs += [jax.ShapeDtypeStruct(kept, F32)] * 2
        scratch += [pltpu.VMEM(kept, F32)] * 3
        sems += [pltpu.SemaphoreType.DMA((ns,))] * 4
        args.append(spec_in)
    vmem = pl.BlockSpec(memory_space=pltpu.VMEM)
    return pl.pallas_call(
        functools.partial(exchange_kernel, n, ns, backward, scale_in, scale_out),
        out_shape=outs,
        in_specs=[vmem] * len(args),
        out_specs=[vmem] * len(outs),
        scratch_shapes=scratch + sems,
        compiler_params=pltpu.CompilerParams(
            vmem_limit_bytes=VMEM_LIMIT, collective_id=int(backward), has_side_effects=True
        ),
    )(*args)


def shards(fields, cotangent, spectral_weight, point_weight, point_bias):
    _, rows, channels, columns = fields.shape
    space = lax.axis_size("space")
    samples = lax.axis_size("sample")
    fwd, inv, depth, depth_inv = [jnp.asarray(t) for t in tables(rows, space)]
    owned = MT * MZ // space
    own_rows = 2 * owned
    all_rows = 2 * MT * MZ
    lanes = channels * XY
    cells = NY * rows
    field = jnp.transpose(fields[0], (1, 0, 2))
    cot = jnp.transpose(cotangent[0], (1, 0, 2))
    flat = channels * rows
    copies = np.repeat(np.eye(channels), rows, 0).astype(BF16)
    same = np.tile(np.eye(rows), (channels, channels)).astype(BF16)
    flat_buf = pltpu.VMEM((flat, flat), BF16)

    freq = np.tile(signed(MX), MY * channels)
    angle = 2 * np.pi * (freq[None, :] * np.arange(space)[:, None] * rows % NX) / NX
    turn_cos = np.cos(angle).astype(np.float32)
    turn_sin = np.sin(angle).astype(np.float32)

    z_buf = pltpu.VMEM((channels, XY, 2 * PLANE), BF16)
    g_buf = pltpu.VMEM((channels, 2 * XY, PLANE), BF16)
    w_buf = pltpu.VMEM((channels, cells, PLANE), F32)
    part = jax.ShapeDtypeStruct((all_rows, lanes), F32)
    grid_bf = jax.ShapeDtypeStruct((channels, rows, columns), BF16)
    grid_f = jax.ShapeDtypeStruct((channels, rows, columns), F32)

    weights = spectral_weight.astype(F32)

    partial = call(first_kernel, part, [w_buf, z_buf, z_buf])(field, fwd, depth)
    split_part = lambda value: value.reshape(space, own_rows, lanes)
    modes, spec_in = exchange(
        split_part(partial), weights, turn_cos, turn_sin, None,
        space, samples, 1.0, 1.0 / VOLUME,
    )
    activated, local, partial_up = call(
        middle_kernel, (grid_bf, grid_f, part), [w_buf, g_buf, g_buf, z_buf, z_buf, flat_buf, flat_buf, pltpu.VMEM((flat, PLANE), F32)]
    )(
        modes.reshape(all_rows, lanes), field, cot, point_weight, point_weight.T,
        point_bias[None], copies, copies.T, same, fwd, inv, depth, depth_inv,
    )
    modes_back, spec_all, up_all = exchange(
        split_part(partial_up), weights, turn_cos, turn_sin, spec_in,
        space, samples, 1.0 / VOLUME, 1.0,
    )
    count = owned * XY // samples
    grad_shape = jax.ShapeDtypeStruct((channels, channels, 2, count), F32)
    grad_input, grad = call(last_kernel, (grid_bf, grad_shape), [w_buf, g_buf, g_buf])(
        modes_back.reshape(all_rows, lanes), local, spec_all, up_all, inv, depth_inv
    )
    grad_spectral = jnp.transpose(grad, (2, 0, 1, 3))
    back_to = lambda value: jnp.transpose(value, (1, 0, 2))[None]
    return back_to(activated), back_to(grad_input), grad_spectral


def solution(mesh):
    return jax.shard_map(
        shards,
        mesh=mesh,
        in_specs=(
            P("sample", "space", None, None),
            P("sample", "space", None, None),
            P(None, None, None, "space"),
            P(),
            P(),
        ),
        out_specs=(
            P("sample", "space", None, None),
            P("sample", "space", None, None),
            P(None, None, None, ("space", "sample")),
        ),
        check_vma=False,
    )
```
